128 devices in a mesh: req: 4 (over y), tm: 32 (over z, x, core).
Axes of the slice: x: 4, y: 4, z: 4, core: 2. Of those that a mesh axis runs over, the one named last changes fastest.
Arguments:
- latents: bfloat16 [128, 12288], P('req', 'tm'), may hold values from -6 to 6
- lengths: int32 [8], replicated, may hold values from 1 to 21, 128 in all
- w_in: bfloat16 [3, 3, 3, 16, 384], replicated, may hold values from -0.3125 to 0.3125
- b_in: float32 [384], replicated, may hold values from -3 to 3
- w_mid: bfloat16 [3, 3, 3, 384, 384], replicated, may hold values from -0.0625 to 0.0625
- b_mid: float32 [384], replicated, may hold values from -3 to 3
Outputs:
- decoded: bfloat16 [128, 64, 48, 384], P(('req', 'tm'))
The draws below stay inside these ranges and needn't reach their ends.
Inputs may be any that keep to these rules, and one draw needn't show every extreme that they name: Request lengths in latent frames, in order along the frames, summing to 128; the longest has exactly 21.
All inputs are finite; a program needn't handle non-finite values.
Results may differ from the reference program's by a relative error of at most 0.0041.
Values may be sent and summed in bfloat16 or wider, within the bound.
No kernel may reach another device: no remote copies, remote signals or barrier semaphores. Data moves between devices by JAX's collectives and lax.ppermute only.
A program may use at most 192 MiB of HBM per device.

```python
import math
import jax
import jax.numpy as jnp
import numpy as np
from jax import lax

C = 16
CH = 384
HT = 32
WT = 24
MOST = 21
FRAMES = 128
REQS = 8


def shard_levels(stream_key, dims, cuts, smallest, largest):
    def one(axis_at, shards_of):
        steps = jax.random.uniform(jax.random.fold_in(jax.random.fold_in(stream_key, 6), axis_at), (shards_of,), jnp.float32, smallest / len(cuts), largest / len(cuts))
        return jnp.repeat(jnp.exp(steps), dims[axis_at] // shards_of).reshape((-1,) + (1,) * (len(dims) - axis_at - 1))

    factor_of = one(*cuts[0])
    for cut in cuts[1:]:
        factor_of = factor_of * one(*cut)
    return factor_of


def profile(amount, total, bound, lean):
    weights = [(1 << 20) // math.isqrt(standing ** lean) + 1 for standing in range(2, amount + 1)]
    spare, given = total - bound - (amount - 1), [1] * (amount - 1)
    while spare > 0:
        free = [i for i in range(amount - 1) if given[i] < bound]
        pool, budget = sum([weights[i] for i in free]), spare
        for i in free:
            more = min(bound - given[i], max(1, budget * weights[i] // pool), spare)
            given[i] = given[i] + more
            spare = spare - more
    return np.array([bound] + given)


def ragged(stream_key, number_of, total, reach, skew):
    if number_of == 2:
        one = jax.random.randint(stream_key, (), max(1, total - reach), min(reach, total - 1) + 1)
        return jnp.stack([one, total - one])
    sizes = jnp.asarray(profile(number_of, total, reach, skew), jnp.int32)
    pairs = (number_of - 1) // 2
    giver, taker = sizes[1:1 + 2 * pairs:2], sizes[2:2 + 2 * pairs:2]
    slack = jnp.minimum(giver - 1, reach - taker)
    moved = jax.random.randint(jax.random.fold_in(stream_key, 1), (pairs,), 0, 1 << 20) % (slack + 1)
    sizes = sizes.at[1:1 + 2 * pairs:2].set(giver - moved).at[2:2 + 2 * pairs:2].set(taker + moved)
    return sizes[jax.random.permutation(jax.random.fold_in(stream_key, 2), number_of)]


def scatter_about(stream_key, shape, deviation, bound, split=(), kind=jnp.bfloat16):
    entries = jax.random.normal(stream_key, shape, jnp.float32) * deviation
    if len(split) > 0:
        entries = shard_levels(stream_key, shape, split, -0.22, 0.18) * entries
    return jnp.clip(entries, min=-bound, max=bound).astype(kind)


def setup_inputs(seed: int = 0) -> dict:
    keys = jax.random.split(jax.random.key(seed), 7)
    latents = scatter_about(keys[0], (FRAMES, HT * WT * C), 1.0, 6.0, ((0, 4), (1, 32)))
    lengths = ragged(keys[1], REQS, FRAMES, MOST, 2).astype(jnp.int32)
    w_in = scatter_about(keys[2], (3, 3, 3, C, CH), (27 * C) ** -0.5, 0.3125)
    b_in = scatter_about(keys[3], (CH,), 0.5, 3.0, (), jnp.float32)
    w_mid = scatter_about(keys[4], (3, 3, 3, CH, CH), (27 * CH) ** -0.5, 0.0625)
    b_mid = scatter_about(keys[5], (CH,), 0.5, 3.0, (), jnp.float32)
    return {"latents": latents, "lengths": lengths, "w_in": w_in, "b_in": b_in, "w_mid": w_mid, "b_mid": b_mid}


def request_of(position, request_ends):
    return jnp.sum((position[:, None] >= request_ends[None, :]).astype(jnp.int32), axis=1)


def keep_taps(position, request_ends):
    own_request = request_of(position, request_ends)
    columns = []
    for offset in (2, 1):
        earlier = position - offset
        matches = (earlier >= 0) & (request_of(earlier, request_ends) == own_request)
        columns.append(matches.astype(jnp.bfloat16))
    columns.append(jnp.ones_like(columns[0]))
    return jnp.stack(columns, axis=1)


def causal_conv(window, tap_mask, weight, bias):
    out_frames = window.shape[0] - 2
    height = window.shape[1] - 2
    breadth = window.shape[2] - 2
    in_chan = window.shape[3]
    out_chan = weight.shape[-1]
    summed = jnp.zeros((out_frames * height * breadth, out_chan), jnp.float32)
    for time_tap in range(3):
        tap_keep = tap_mask[:, time_tap][:, None, None, None]
        for row_tap in range(3):
            columns = jnp.concatenate(
                [window[time_tap:time_tap + out_frames, row_tap:row_tap + height, col_tap:col_tap + breadth, :]
                 for col_tap in range(3)], axis=-1) * tap_keep
            summed = summed + jnp.dot(columns.reshape(out_frames * height * breadth, 3 * in_chan),
                                      weight[time_tap, row_tap].reshape(3 * in_chan, out_chan),
                                      preferred_element_type=jnp.float32)
    return (summed + bias[None, :]).reshape(out_frames, height, breadth, out_chan)


def upsample(field):
    return jnp.repeat(jnp.repeat(field, 2, axis=1), 2, axis=2)


def run_conv(frames_all, tap_mask, weight, bias):
    padded = jnp.pad(frames_all, ((2, 0), (1, 1), (1, 1), (0, 0)))

    def one_frame(index):
        window = lax.dynamic_slice_in_dim(padded, index, 3, 0)
        taps = lax.dynamic_slice_in_dim(tap_mask, index, 1, 0)
        return causal_conv(window, taps, weight, bias)[0]

    return lax.map(one_frame, jnp.arange(frames_all.shape[0], dtype=jnp.int32))


def reference(latents, lengths, w_in, b_in, w_mid, b_mid):
    latent = latents.reshape(FRAMES, HT, WT, C)
    request_ends = jnp.cumsum(lengths).astype(jnp.int32)
    tap_mask = keep_taps(jnp.arange(FRAMES, dtype=jnp.int32), request_ends)
    hidden = jax.nn.silu(run_conv(latent, tap_mask, w_in, b_in)).astype(jnp.bfloat16)
    decoded = run_conv(upsample(hidden), tap_mask, w_mid, b_mid)
    return decoded.astype(jnp.bfloat16)
```

```python
import jax
import jax.numpy as jnp
from jax import lax
from jax.experimental import pallas as pl
from jax.experimental.pallas import tpu as pltpu
from jax.sharding import PartitionSpec as P

C = 16
HT = 32
WT = 24
CH = 384
BF = jnp.bfloat16
F32 = jnp.float32
KIN = 27 * C
KMID = 3 * CH
JC = 8
VMEM_LIMIT = 56 * 2**20


def prep_body(w_ref, o_ref):
    w = [[w_ref[0, p, q].astype(F32) for q in range(3)] for p in range(3)]
    by_row = []
    for p in range(3):
        by_row.append((w[p][0] + w[p][1] + w[p][2], w[p][0], w[p][2]))
    rows = lambda k: by_row[0][k] + by_row[1][k] + by_row[2][k]
    parts = [rows(0), rows(1), rows(2)]
    parts += [by_row[0][0], by_row[2][0]]
    parts += [by_row[0][1], by_row[0][2], by_row[2][1], by_row[2][2]]
    for k, part in enumerate(parts):
        o_ref[:, k * CH : (k + 1) * CH] = part.astype(BF)


def prep(w_mid):
    rows = 128
    per = CH // rows
    return pl.pallas_call(
        prep_body,
        grid=(3 * per,),
        in_specs=[
            pl.BlockSpec((1, 3, 3, rows, CH), lambda n: (n // per, 0, 0, n % per, 0))
        ],
        out_specs=pl.BlockSpec((rows, 9 * CH), lambda n: (n, 0)),
        out_shape=jax.ShapeDtypeStruct((KMID, 9 * CH), BF),
        compiler_params=pltpu.CompilerParams(vmem_limit_bytes=24 * 2**20),
        name="prep",
    )(w_mid)


def main_body(
    pos_ref, len_ref, x_ref, win_ref, bin_ref, bmid_ref, wt_hbm, out_hbm,
    xf, zt, at, hf, hb, dc, dr, dd, wt, r_ss, r_ds, r_sd, r_dd, st, ob, wsem, osem,
):
    nparts = 3
    wrows = KMID // nparts
    copies = []
    for k in range(nparts):
        cp = pltpu.make_async_copy(
            wt_hbm.at[pl.ds(k * wrows, wrows)], wt.at[pl.ds(k * wrows, wrows)], wsem.at[k]
        )
        cp.start()
        copies.append(cp)

    first = pos_ref[0] - 4
    rid = [jnp.int32(0)] * 5
    end = jnp.int32(0)
    for r in range(8):
        end = end + len_ref[r]
        rid = [rid[k] + (first + k >= end).astype(jnp.int32) for k in range(5)]
    ok = lambda k, g: ((first + k >= 0) & (rid[k] == rid[g])).astype(F32)
    m_in = [[ok(g + t, g + 2) if t < 2 else jnp.float32(1) for t in range(3)] for g in range(3)]
    m_mid = [ok(2, 4), ok(3, 4), jnp.float32(1)]

    xf[0:16, :] = jnp.zeros((16, 128), F32)
    xf[33 * 16 : 34 * 16, :] = jnp.zeros((16, 128), F32)
    xf[16 : 33 * 16, :] = x_ref[...].reshape(HT * 16, 128).astype(F32)

    for t in range(3):
        for p in range(3):
            zt[3 * t + p, 0:16, :] = jnp.zeros((16, 128), BF)
            zt[3 * t + p, 16 + CH : 32 + CH, :] = jnp.zeros((16, 128), BF)
            for c3 in range(3):
                block = [
                    xf[pl.ds(p * 16 + (g + t) * 3 + c3, HT, stride=16), :] * m_in[g][t]
                    for g in range(3)
                ]
                block.append(jnp.zeros((HT, 128), F32))
                z = jnp.concatenate(block, axis=0)
                zt[3 * t + p, 16 + c3 * 128 : 16 + (c3 + 1) * 128, :] = z.T.astype(BF)

    for tp in range(9):
        for j in range(WT):
            at[tp * 48 : (tp + 1) * 48, j * 128 : (j + 1) * 128] = zt[tp, 16 * j : 16 * j + 48, :]

    def conv_in(n, carry):
        a = at[:, pl.ds(pl.multiple_of(n * JC * 128, 128), JC * 128)]
        v = lax.dot_general(a, win_ref[...], (((0,), (0,)), ((), ())), preferred_element_type=F32)
        v = v + bin_ref[...]
        s = (0.5 * v) * (1.0 + jnp.tanh(0.5 * v))
        s = s.reshape(JC, 128, CH)
        for g in range(3):
            hg = (s[:, 32 * g : 32 * g + 32, :].reshape(JC * HT, CH) * m_mid[g]).astype(BF)
            base = pl.multiple_of(n * JC * HT, 256)
            hb[pl.ds(base, JC * HT), g * CH : (g + 1) * CH] = hg
            hgf = hg.astype(F32)
            for c3 in range(3):
                hf[g * 3 + c3, pl.ds(base + 8, JC * HT), :] = hgf[:, c3 * 128 : (c3 + 1) * 128]
        return carry

    for n in range(WT // JC):
        conv_in(n, 0)

    dc[0:HT, :] = hb[0:HT, :]
    dc[HT : WT * HT, :] = hb[HT : WT * HT, :] - hb[0 : (WT - 1) * HT, :]
    dc[WT * HT : (WT + 1) * HT, :] = -hb[(WT - 1) * HT : WT * HT, :]

    def row_diff(k, carry):
        here = hf[k, pl.ds(8, WT * HT), :]
        above = hf[k, pl.ds(7, WT * HT), :]
        top = lax.broadcasted_iota(jnp.int32, (WT * HT, 128), 0) % HT == 0
        lanes = pl.ds(pl.multiple_of(k * 128, 128), 128)
        dr[0 : WT * HT, lanes] = (here - jnp.where(top, 0.0, above)).astype(BF)
        last = hf[k, pl.ds(8 + HT - 1, WT, stride=HT), :]
        dr[WT * HT : WT * HT + 32, lanes] = jnp.concatenate([-last, jnp.zeros((8, 128), F32)], axis=0).astype(BF)
        prev = jnp.concatenate([jnp.zeros((1, 128), F32), last, jnp.zeros((7, 128), F32)], axis=0)
        cur = jnp.concatenate([last, jnp.zeros((8, 128), F32)], axis=0)
        dd[(WT + 1) * HT : (WT + 1) * HT + 32, lanes] = (prev - cur).astype(BF)
        return carry

    for k in range(9):
        row_diff(k, 0)
    dd[0:HT, :] = dr[0:HT, :]
    dd[HT : WT * HT, :] = dr[HT : WT * HT, :] - dr[0 : (WT - 1) * HT, :]
    dd[WT * HT : (WT + 1) * HT, :] = -dr[(WT - 1) * HT : WT * HT, :]

    for cp in copies:
        cp.wait()
    def mm(out, lhs, lo, hi):
        v = jnp.dot(lhs[...], wt[:, lo * CH : hi * CH], preferred_element_type=F32)
        for k in range(3 * (hi - lo)):
            part = v[:, k * 128 : (k + 1) * 128]
            out[k] = part + bmid_ref[:, k * 128 : (k + 1) * 128] if lo == 0 else part

    mm(r_ss, hb, 0, 1)
    mm(r_ds, dc, 1, 3)
    mm(r_sd, dr, 3, 5)
    mm(r_dd, dd, 5, 9)

    def emit(i, start, step):
        for c in range(3):
            here = pl.ds(i, WT, stride=HT)
            right = pl.ds(i + HT, WT, stride=HT)
            below = pl.ds(start, WT, stride=step)
            dstart = start + (HT if step == 1 else 0)
            dbelow = pl.ds(dstart, WT, stride=step)
            dright = pl.ds(dstart + step, WT, stride=step)
            ss = r_ss[c, here, :]
            t0 = ss - r_ds[c, here, :]
            t1 = ss + r_ds[3 + c, right, :]
            above = r_sd[c, here, :]
            under = r_sd[3 + c, below, :]
            st[c, 0, pl.ds(0, WT, stride=2), :] = t0 - (above - r_dd[c, here, :])
            st[c, 0, pl.ds(1, WT, stride=2), :] = t1 - (above + r_dd[3 + c, right, :])
            st[c, 1, pl.ds(0, WT, stride=2), :] = t0 + (under - r_dd[6 + c, dbelow, :])
            st[c, 1, pl.ds(1, WT, stride=2), :] = t1 + (under + r_dd[9 + c, dright, :])
            for a in range(2):
                ob[2 * i + a, :, c * 128 : (c + 1) * 128] = st[c, a].astype(BF)

    def step(i, carry):
        emit(i, i + 1, HT)
        pltpu.make_async_copy(ob.at[pl.ds(2 * i, 2)], out_hbm.at[0, pl.ds(2 * i, 2)], osem).start()
        return carry

    lax.fori_loop(0, HT - 1, step, 0)
    emit(HT - 1, WT * HT, 1)
    pltpu.make_async_copy(ob.at[pl.ds(2 * HT - 2, 2)], out_hbm.at[0, pl.ds(2 * HT - 2, 2)], osem).start()
    pltpu.make_async_copy(ob, out_hbm.at[0], osem).wait()


def decode(pos, lengths, x, w_in, b_in, b_mid, wt):
    smem = pl.BlockSpec(memory_space=pltpu.SMEM)
    vmem = pl.BlockSpec(memory_space=pltpu.VMEM)
    hbm = pl.BlockSpec(memory_space=pl.ANY)
    n = WT * HT
    return pl.pallas_call(
        main_body,
        in_specs=[smem, smem, vmem, vmem, vmem, vmem, hbm],
        out_specs=hbm,
        out_shape=jax.ShapeDtypeStruct((1, 2 * HT, 2 * WT, CH), BF),
        scratch_shapes=[
            pltpu.VMEM((34 * 16, 128), F32),
            pltpu.VMEM((9, CH + 32, 128), BF),
            pltpu.VMEM((KIN, WT * 128), BF),
            pltpu.VMEM((9, n + 16, 128), F32),
            pltpu.VMEM((n, KMID), BF),
            pltpu.VMEM((n + HT, KMID), BF),
            pltpu.VMEM((n + 32, KMID), BF),
            pltpu.VMEM((n + HT + 32, KMID), BF),
            pltpu.VMEM((KMID, 9 * CH), BF),
            pltpu.VMEM((3, n, 128), F32),
            pltpu.VMEM((6, n + HT, 128), F32),
            pltpu.VMEM((6, n + 32, 128), F32),
            pltpu.VMEM((12, n + HT + 32, 128), F32),
            pltpu.VMEM((3, 2, 2 * WT, 128), F32),
            pltpu.VMEM((2 * HT, 2 * WT, CH), BF),
            pltpu.SemaphoreType.DMA((3,)),
            pltpu.SemaphoreType.DMA,
        ],
        compiler_params=pltpu.CompilerParams(vmem_limit_bytes=VMEM_LIMIT),
        name="decode",
    )(pos, lengths, x, w_in, b_in, b_mid, wt)


def on_device(latents, lengths, w_in, b_in, w_mid, b_mid):
    group = lax.axis_size("req")
    peers = lax.axis_size("tm")
    before = lax.ppermute(latents[peers - 4 :], "req", [(i, i + 1) for i in range(group - 1)])
    rows = jnp.concatenate([before, latents], axis=0)
    slots = jnp.stack([rows[k : k + peers] for k in range(5)], axis=1)
    slots = slots.reshape(peers, 15, 128)
    slots = jnp.pad(slots, ((0, 0), (0, 1), (0, 0)))
    x = lax.all_to_all(slots, "tm", split_axis=0, concat_axis=0, tiled=True)
    wt = prep(w_mid)
    pos = lax.axis_index(("req", "tm")).astype(jnp.int32).reshape(1)
    return decode(
        pos, lengths, x, w_in.reshape(KIN, CH), b_in.reshape(1, CH), b_mid.reshape(1, CH), wt
    )


def solution(mesh):
    in_specs = (P("req", "tm"), P(), P(), P(), P(), P())
    out_specs = P(("req", "tm"), None, None, None)
    return jax.shard_map(
        on_device, mesh=mesh, in_specs=in_specs, out_specs=out_specs, check_vma=False
    )
```

```python
import jax
import jax.numpy as jnp
from jax import lax
from jax.experimental import pallas as pl
from jax.experimental.pallas import tpu as pltpu
from jax.sharding import PartitionSpec as P

C = 16
HT = 32
WT = 24
CH = 384
BF = jnp.bfloat16
F32 = jnp.float32
KIN = 27 * C
KMID = 3 * CH
SUMS = (1, 2, 2)
STRIP = 4
SW = WT // STRIP
VMEM_LIMIT = 44 * 2**20
PITCH = WT + 1
TOP = 32
MROW = 832


def prep_body(w_ref, ss_ref, ds_ref, sd_ref):
    w = [[w_ref[0, p, q].astype(F32) for q in range(3)] for p in range(3)]
    by_row = []
    for p in range(3):
        by_row.append((w[p][0] + w[p][1] + w[p][2], w[p][0], w[p][2]))
    rows = lambda k: by_row[0][k] + by_row[1][k] + by_row[2][k]
    ss_ref[...] = rows(0).astype(BF)
    ds_ref[:, 0:CH] = rows(1).astype(BF)
    ds_ref[:, CH : 2 * CH] = rows(2).astype(BF)
    sd_ref[:, 0:CH] = by_row[0][0].astype(BF)
    sd_ref[:, CH : 2 * CH] = by_row[2][0].astype(BF)


def prep(w_mid):
    rows = 128
    per = CH // rows
    return pl.pallas_call(
        prep_body,
        grid=(3 * per,),
        in_specs=[
            pl.BlockSpec((1, 3, 3, rows, CH), lambda n: (n // per, 0, 0, n % per, 0))
        ],
        out_specs=[pl.BlockSpec((rows, k * CH), lambda n: (n, 0)) for k in SUMS],
        out_shape=[pltpu.HBM((KMID, k * CH), BF) for k in SUMS],
        compiler_params=pltpu.CompilerParams(vmem_limit_bytes=16 * 2**20),
        name="prep",
    )(w_mid)


def slots_body(before_ref, own_ref, o_ref, rows, out):
    for c in range(3):
        lanes = slice(c * 128, (c + 1) * 128)
        rows[c, 0:8, :] = before_ref[:, lanes].astype(F32)[HT - 8 : HT]
        rows[c, 8 : 8 + HT, :] = own_ref[:, lanes].astype(F32)
        for k in range(8):
            piece = rows[c, 4 + k : 4 + k + HT, :] if k < 5 else jnp.zeros((HT, 128), F32)
            out[c, pl.ds(k, HT, stride=8), :] = piece
        o_ref[:, :, lanes] = out[c].reshape(HT, 8, 128).astype(BF)


def slots(before, own):
    return pl.pallas_call(
        slots_body,
        out_shape=jax.ShapeDtypeStruct((HT, 8, CH), BF),
        scratch_shapes=[pltpu.VMEM((3, HT + 8, 128), F32), pltpu.VMEM((3, HT * 8, 128), F32)],
        compiler_params=pltpu.CompilerParams(vmem_limit_bytes=8 * 2**20),
        name="slots",
    )(before, own)


def main_body(
    pos_ref, len_ref, x_ref, win_ref, bin_ref, bmid_ref, ss_hbm, ds_hbm, sd_hbm, w_hbm, out_hbm,
    xf, xp, zt, at, hf, hb, dc, dr, dd, w_ss, w_ds, w_sd, w_dd, r_ss, r_ds, r_sd, r_dd, st, ob, wsem, osem,
):
    sums = [
        pltpu.make_async_copy(src, dst, wsem.at[k])
        for k, (src, dst) in enumerate(((ss_hbm, w_ss), (ds_hbm, w_ds), (sd_hbm, w_sd)))
    ]
    outer = [
        pltpu.make_async_copy(w_hbm.at[t, p, q], w_dd.at[k, pl.ds(t * CH, CH)], wsem.at[3 + 3 * k + t])
        for k, (p, q) in enumerate(((0, 0), (0, 2), (2, 0), (2, 2)))
        for t in range(3)
    ]
    for cp in sums + outer:
        cp.start()

    first = pos_ref[0] - 4
    rid = [jnp.int32(0)] * 5
    end = jnp.int32(0)
    for r in range(8):
        end = end + len_ref[r]
        rid = [rid[k] + (first + k >= end).astype(jnp.int32) for k in range(5)]
    ok = lambda k, g: ((first + k >= 0) & (rid[k] == rid[g])).astype(F32)
    m_in = [[ok(g + t, g + 2) if t < 2 else None for t in range(3)] for g in range(3)]
    m_mid = [ok(2, 4), ok(3, 4), None]
    bias = lambda ref, c: ref[pl.ds(c * 128, 128)].reshape(1, 128)
    times = lambda v, m: v if m is None else v * m

    for c in range(3):
        xf[c] = x_ref[:, :, c * 128 : (c + 1) * 128].reshape(HT * 8, 128).astype(F32)
    for f in range(5):
        x = [xf[c, pl.ds(f, HT, stride=8), :] for c in range(3)]
        x = jnp.concatenate([jnp.zeros((HT, C), F32)] + x + [jnp.zeros((HT, 128 - C), F32)], axis=1)
        for s in range(STRIP):
            k = f * STRIP + s
            xp[k, 0:8, :] = jnp.zeros((8, 128), F32)
            xp[k, 8 : 8 + HT, :] = x[:, s * SW * C : s * SW * C + 128]
            xp[k, 8 + HT : 16 + HT, :] = jnp.zeros((8, 128), F32)

    for t in range(3):
        for p in range(3):
            for b in range(3):
                block = []
                for k in range(4 * b, 4 * b + 4):
                    s, g = k // 3, k % 3
                    block.append(times(xp[(g + t) * STRIP + s, 7 + p : 7 + p + HT, :], m_in[g][t]))
                z = jnp.concatenate(block, axis=0)
                zt[3 * t + p, :, b * 128 : (b + 1) * 128] = z.T.astype(BF)

    for tp in range(9):
        for j in range(SW):
            at[tp * 48 : (tp + 1) * 48, j * CH : (j + 1) * CH] = zt[tp, 16 * j : 16 * j + 48, :]

    for k in range(9):
        hf[k, 0:TOP, :] = jnp.zeros((TOP, 128), F32)
        hf[k, pl.ds(TOP + WT, HT, stride=PITCH), :] = jnp.zeros((HT, 128), F32)
        hf[k, TOP + HT * PITCH : TOP + MROW, :] = jnp.zeros((MROW - HT * PITCH, 128), F32)

    for n in range(SW // 2):
        a = at[:, n * 2 * CH : (n + 1) * 2 * CH]
        v = lax.dot_general(a, win_ref[...], (((0,), (0,)), ((), ())), preferred_element_type=F32)
        for k in range(2 * STRIP * 3):
            s, g, j = k // 3 % STRIP, k % 3, n * 2 + k // (3 * STRIP)
            for c in range(3):
                u = v[k * HT : (k + 1) * HT, c * 128 : (c + 1) * 128]
                u = 0.5 * (u + bias(bin_ref, c))
                u = times(u * (1.0 + jnp.tanh(u)), m_mid[g]).astype(BF).astype(F32)
                hf[3 * g + c, pl.ds(TOP + s * SW + j, HT, stride=PITCH), :] = u

    for cp in sums + outer:
        cp.wait()

    half = MROW // 2
    for k in range(9):
        lanes = slice(k * 128, (k + 1) * 128)
        for lo in range(0, MROW, half):
            rows = slice(lo, lo + half)
            h = lambda back: hf[k, TOP + lo - back : TOP + lo + half - back, :]
            col = h(0) - h(1)
            hb[rows, lanes] = h(0).astype(BF)
            dc[rows, lanes] = col.astype(BF)
            dr[rows, lanes] = (h(0) - h(PITCH)).astype(BF)
            dd[rows, lanes] = (col - (h(PITCH) - h(PITCH + 1))).astype(BF)

    def mm(out, lhs, rows, w):
        v = jnp.dot(lhs[0:rows, :], w, preferred_element_type=F32)
        for k in range(v.shape[1] // 128):
            part = v[:, k * 128 : (k + 1) * 128]
            out[k] = part + bias(bmid_ref, k) if out is r_ss else part

    mm(r_ss, hb, HT * PITCH, w_ss[...])
    mm(r_ds, dc, HT * PITCH, w_ds[...])
    mm(r_sd, dr, MROW, w_sd[...])

    mm(r_dd, dd, MROW, jnp.concatenate([w_dd[k] for k in range(4)], axis=1))

    def emit(i, c):
        at_row = lambda ref, k, off: ref[k, i * PITCH + off : i * PITCH + off + WT, :]
        slot = i % 4
        ss = at_row(r_ss, c, 0)
        t0 = ss - at_row(r_ds, c, 0)
        t1 = ss + at_row(r_ds, 3 + c, 1)
        above = at_row(r_sd, c, 0)
        under = at_row(r_sd, 3 + c, PITCH)
        st[c, slot, 0, pl.ds(0, WT, stride=2), :] = t0 - (above - at_row(r_dd, c, 0))
        st[c, slot, 0, pl.ds(1, WT, stride=2), :] = t1 - (above + at_row(r_dd, 3 + c, 1))
        st[c, slot, 1, pl.ds(0, WT, stride=2), :] = t0 + (under - at_row(r_dd, 6 + c, PITCH))
        st[c, slot, 1, pl.ds(1, WT, stride=2), :] = t1 + (under + at_row(r_dd, 9 + c, PITCH + 1))
        for a in range(2):
            ob[2 * i + a, :, c * 128 : (c + 1) * 128] = st[c, slot, a].astype(BF)

    for i in range(HT):
        for c in range(3):
            emit(i, c)
        if i % 8 == 7:
            block = pl.ds(2 * (i - 7), 16)
            pltpu.make_async_copy(ob.at[block], out_hbm.at[0, block], osem).start()
    pltpu.make_async_copy(ob, out_hbm.at[0], osem).wait()


def decode(pos, lengths, x, w_in, b_in, b_mid, ss, ds, sd, w_mid):
    smem = pl.BlockSpec(memory_space=pltpu.SMEM)
    vmem = pl.BlockSpec(memory_space=pltpu.VMEM)
    hbm = pl.BlockSpec(memory_space=pl.ANY)
    return pl.pallas_call(
        main_body,
        in_specs=[smem, smem, vmem, vmem, vmem, vmem, hbm, hbm, hbm, hbm],
        out_specs=hbm,
        out_shape=jax.ShapeDtypeStruct((1, 2 * HT, 2 * WT, CH), BF),
        scratch_shapes=[
            pltpu.VMEM((3, HT * 8, 128), F32),
            pltpu.VMEM((5 * STRIP, HT + 16, 128), F32),
            pltpu.VMEM((9, 128, CH), BF),
            pltpu.VMEM((KIN, SW * CH), BF),
            pltpu.VMEM((9, TOP + MROW, 128), F32),
            pltpu.VMEM((MROW, KMID), BF),
            pltpu.VMEM((MROW, KMID), BF),
            pltpu.VMEM((MROW, KMID), BF),
            pltpu.VMEM((MROW, KMID), BF),
            pltpu.VMEM((KMID, CH), BF),
            pltpu.VMEM((KMID, 2 * CH), BF),
            pltpu.VMEM((KMID, 2 * CH), BF),
            pltpu.VMEM((4, KMID, CH), BF),
            pltpu.VMEM((3, HT * PITCH, 128), F32),
            pltpu.VMEM((6, HT * PITCH, 128), F32),
            pltpu.VMEM((6, MROW, 128), F32),
            pltpu.VMEM((12, MROW, 128), F32),
            pltpu.VMEM((3, 4, 2, 2 * WT, 128), F32),
            pltpu.VMEM((2 * HT, 2 * WT, CH), BF),
            pltpu.SemaphoreType.DMA((15,)),
            pltpu.SemaphoreType.DMA,
        ],
        compiler_params=pltpu.CompilerParams(vmem_limit_bytes=VMEM_LIMIT),
        name="decode",
    )(pos, lengths, x, w_in, b_in, b_mid, ss, ds, sd, w_mid)


def on_device(latents, lengths, w_in, b_in, w_mid, b_mid):
    groups = lax.axis_size("req")
    before = lax.ppermute(latents, "req", [(i, i + 1) for i in range(groups - 1)])
    x = lax.all_to_all(slots(before, latents), "tm", split_axis=0, concat_axis=0, tiled=True)
    w_mid = pltpu.with_memory_space_constraint(w_mid, pltpu.HBM)
    sums = [pltpu.with_memory_space_constraint(w, pltpu.HBM) for w in prep(w_mid)]
    pos = lax.axis_index(("req", "tm")).astype(jnp.int32).reshape(1)
    return decode(pos, lengths, x, w_in.reshape(KIN, CH), b_in, b_mid, *sums, w_mid)


def solution(mesh):
    in_specs = (P("req", "tm"), P(), P(), P(), P(), P())
    out_specs = P(("req", "tm"), None, None, None)
    return jax.shard_map(
        on_device, mesh=mesh, in_specs=in_specs, out_specs=out_specs, check_vma=False
    )
```

```python
import jax
import jax.numpy as jnp
from jax import lax
from jax.experimental import pallas as pl
from jax.experimental.pallas import tpu as pltpu
from jax.sharding import PartitionSpec as P

C = 16
HT = 32
WT = 24
CH = 384
BF = jnp.bfloat16
F32 = jnp.float32
KIN = 27 * C
KMID = 3 * CH
STRIP = 4
SW = WT // STRIP
VMEM_LIMIT = 44 * 2**20
PITCH = WT + 1
TOP = 32
MROW = 832


def prep_body(w_hbm, ss_ref, ds_ref, sd_hbm, w, sd, isem, osem):
    rows = 128
    parts = [(t, slice(r, r + rows)) for t in range(3) for r in range(0, CH, rows)]
    reads, writes = [], []
    for n, (t, r) in enumerate(parts):
        cp = pltpu.make_async_copy(w_hbm.at[t, :, :, r], w.at[t, :, :, r], isem.at[n])
        cp.start()
        reads.append(cp)
    for n, (t, r) in enumerate(parts):
        reads[n].wait()
        out = slice(n * rows, (n + 1) * rows)
        tap = lambda p, q: w[t, p, q, r].astype(F32)
        col = [[tap(p, q) for p in range(3)] for q in range(3)]
        col_sum = [c[0] + c[1] + c[2] for c in col]
        ss_ref[out] = (col_sum[0] + col_sum[1] + col_sum[2]).astype(BF)
        ds_ref[out, 0:CH] = col_sum[0].astype(BF)
        ds_ref[out, CH : 2 * CH] = col_sum[2].astype(BF)
        sd[out, 0:CH] = (col[0][0] + col[1][0] + col[2][0]).astype(BF)
        sd[out, CH : 2 * CH] = (col[0][2] + col[1][2] + col[2][2]).astype(BF)
        cp = pltpu.make_async_copy(sd.at[out], sd_hbm.at[out], osem.at[n])
        cp.start()
        writes.append(cp)
    for cp in writes:
        cp.wait()


def prep(w_mid):
    vmem = pl.BlockSpec(memory_space=pltpu.VMEM)
    hbm = pl.BlockSpec(memory_space=pl.ANY)
    return pl.pallas_call(
        prep_body,
        in_specs=[hbm],
        out_specs=[vmem, vmem, hbm],
        out_shape=[
            jax.ShapeDtypeStruct((KMID, CH), BF),
            jax.ShapeDtypeStruct((KMID, 2 * CH), BF),
            pltpu.HBM((KMID, 2 * CH), BF),
        ],
        scratch_shapes=[
            pltpu.VMEM((3, 3, 3, CH, CH), BF),
            pltpu.VMEM((KMID, 2 * CH), BF),
            pltpu.SemaphoreType.DMA((9,)),
            pltpu.SemaphoreType.DMA((9,)),
        ],
        compiler_params=pltpu.CompilerParams(vmem_limit_bytes=20 * 2**20),
        name="prep",
    )(w_mid)


def slots_body(own_ref, o_ref, rows, out):
    for c in range(3):
        lanes = slice(c * 128, (c + 1) * 128)
        rows[c, 0:8, :] = jnp.zeros((8, 128), F32)
        rows[c, 8 : 8 + HT, :] = own_ref[:, lanes].astype(F32)
        for k in range(8):
            piece = rows[c, 4 + k : 4 + k + HT, :] if k < 5 else jnp.zeros((HT, 128), F32)
            out[c, pl.ds(k, HT, stride=8), :] = piece
        o_ref[:, :, lanes] = out[c].reshape(HT, 8, 128).astype(BF)


def slots(own):
    return pl.pallas_call(
        slots_body,
        out_shape=jax.ShapeDtypeStruct((HT, 8, CH), BF),
        scratch_shapes=[pltpu.VMEM((3, HT + 8, 128), F32), pltpu.VMEM((3, HT * 8, 128), F32)],
        compiler_params=pltpu.CompilerParams(vmem_limit_bytes=8 * 2**20),
        name="slots",
    )(own)


def patch_body(before_ref, s_ref, o_ref):
    tail = before_ref[...].astype(F32)[HT - 8 : HT]
    for d in range(4):
        here = s_ref[d].astype(F32)
        o_ref[d] = jnp.concatenate([tail[4 + d : 8], here[4 - d : 8]], axis=0).astype(BF)


def patch(before, own_slots):
    block = pl.BlockSpec((4, 8, CH), lambda n: (0, 0, 0))
    return pl.pallas_call(
        patch_body,
        grid=(1,),
        in_specs=[pl.BlockSpec((HT, CH), lambda n: (0, 0)), block],
        out_specs=block,
        out_shape=jax.ShapeDtypeStruct((HT, 8, CH), BF),
        input_output_aliases={1: 0},
        compiler_params=pltpu.CompilerParams(vmem_limit_bytes=8 * 2**20),
        name="patch",
    )(before, own_slots)


def main_body(
    pos_ref, len_ref, x_ref, win_ref, bin_ref, bmid_ref, w_ss, w_ds, sd_hbm, w_hbm, out_hbm,
    xf, xp, zt, at, hf, hb, dc, dr, dd, w_sd, w_dd, r_ss, r_ds, r_sd, r_dd, st, ob, wsem, osem,
):
    row_sums = pltpu.make_async_copy(sd_hbm, w_sd, wsem.at[0])
    outer = [
        pltpu.make_async_copy(w_hbm.at[t, p, q], w_dd.at[k, pl.ds(t * CH, CH)], wsem.at[1 + 3 * k + t])
        for k, (p, q) in enumerate(((0, 0), (0, 2), (2, 0), (2, 2)))
        for t in range(3)
    ]
    for cp in [row_sums] + outer:
        cp.start()

    first = pos_ref[0] - 4
    rid = [jnp.int32(0)] * 5
    end = jnp.int32(0)
    for r in range(8):
        end = end + len_ref[r]
        rid = [rid[k] + (first + k >= end).astype(jnp.int32) for k in range(5)]
    ok = lambda k, g: ((first + k >= 0) & (rid[k] == rid[g])).astype(F32)
    m_in = [[ok(g + t, g + 2) if t < 2 else None for t in range(3)] for g in range(3)]
    m_mid = [ok(2, 4), ok(3, 4), None]
    bias = lambda ref, c: ref[pl.ds(c * 128, 128)].reshape(1, 128)
    times = lambda v, m: v if m is None else v * m

    for c in range(3):
        xf[c] = x_ref[:, :, c * 128 : (c + 1) * 128].reshape(HT * 8, 128).astype(F32)
    for f in range(5):
        x = [xf[c, pl.ds(f, HT, stride=8), :] for c in range(3)]
        x = jnp.concatenate([jnp.zeros((HT, C), F32)] + x + [jnp.zeros((HT, 128 - C), F32)], axis=1)
        for s in range(STRIP):
            k = f * STRIP + s
            xp[k, 0:8, :] = jnp.zeros((8, 128), F32)
            xp[k, 8 : 8 + HT, :] = x[:, s * SW * C : s * SW * C + 128]
            xp[k, 8 + HT : 16 + HT, :] = jnp.zeros((8, 128), F32)

    for t in range(3):
        for p in range(3):
            for b in range(3):
                block = []
                for k in range(4 * b, 4 * b + 4):
                    s, g = k // 3, k % 3
                    block.append(times(xp[(g + t) * STRIP + s, 7 + p : 7 + p + HT, :], m_in[g][t]))
                z = jnp.concatenate(block, axis=0)
                zt[3 * t + p, :, b * 128 : (b + 1) * 128] = z.T.astype(BF)

    for tp in range(9):
        for j in range(SW):
            at[tp * 48 : (tp + 1) * 48, j * CH : (j + 1) * CH] = zt[tp, 16 * j : 16 * j + 48, :]

    for k in range(9):
        hf[k, 0:TOP, :] = jnp.zeros((TOP, 128), F32)
        hf[k, pl.ds(TOP + WT, HT, stride=PITCH), :] = jnp.zeros((HT, 128), F32)
        hf[k, TOP + HT * PITCH : TOP + MROW, :] = jnp.zeros((MROW - HT * PITCH, 128), F32)

    for n in range(SW // 2):
        a = at[:, n * 2 * CH : (n + 1) * 2 * CH]
        v = lax.dot_general(a, win_ref[...], (((0,), (0,)), ((), ())), preferred_element_type=F32)
        for k in range(2 * STRIP * 3):
            s, g, j = k // 3 % STRIP, k % 3, n * 2 + k // (3 * STRIP)
            for c in range(3):
                u = v[k * HT : (k + 1) * HT, c * 128 : (c + 1) * 128]
                u = 0.5 * (u + bias(bin_ref, c))
                u = times(u * (1.0 + jnp.tanh(u)), m_mid[g]).astype(BF).astype(F32)
                hf[3 * g + c, pl.ds(TOP + s * SW + j, HT, stride=PITCH), :] = u

    row_sums.wait()
    half = MROW // 2
    for k in range(9):
        lanes = slice(k * 128, (k + 1) * 128)
        for lo in range(0, MROW, half):
            rows = slice(lo, lo + half)
            h = lambda back: hf[k, TOP + lo - back : TOP + lo + half - back, :]
            col = h(0) - h(1)
            hb[rows, lanes] = h(0).astype(BF)
            dc[rows, lanes] = col.astype(BF)
            dr[rows, lanes] = (h(0) - h(PITCH)).astype(BF)
            dd[rows, lanes] = (col - (h(PITCH) - h(PITCH + 1))).astype(BF)

    def mm(out, lhs, rows, w):
        v = jnp.dot(lhs[0:rows, :], w, preferred_element_type=F32)
        for k in range(v.shape[1] // 128):
            part = v[:, k * 128 : (k + 1) * 128]
            out[k] = part + bias(bmid_ref, k) if out is r_ss else part

    mm(r_ss, hb, HT * PITCH, w_ss[...])
    mm(r_ds, dc, HT * PITCH, w_ds[...])
    mm(r_sd, dr, MROW, w_sd[...])

    for cp in outer:
        cp.wait()
    mm(r_dd, dd, MROW, jnp.concatenate([w_dd[k] for k in range(4)], axis=1))

    def emit(i, c):
        at_row = lambda ref, k, off: ref[k, i * PITCH + off : i * PITCH + off + WT, :]
        slot = i % 4
        ss = at_row(r_ss, c, 0)
        t0 = ss - at_row(r_ds, c, 0)
        t1 = ss + at_row(r_ds, 3 + c, 1)
        above = at_row(r_sd, c, 0)
        under = at_row(r_sd, 3 + c, PITCH)
        st[c, slot, 0, pl.ds(0, WT, stride=2), :] = t0 - (above - at_row(r_dd, c, 0))
        st[c, slot, 0, pl.ds(1, WT, stride=2), :] = t1 - (above + at_row(r_dd, 3 + c, 1))
        st[c, slot, 1, pl.ds(0, WT, stride=2), :] = t0 + (under - at_row(r_dd, 6 + c, PITCH))
        st[c, slot, 1, pl.ds(1, WT, stride=2), :] = t1 + (under + at_row(r_dd, 9 + c, PITCH + 1))
        for a in range(2):
            ob[2 * i + a, :, c * 128 : (c + 1) * 128] = st[c, slot, a].astype(BF)

    for i in range(HT):
        for c in range(3):
            emit(i, c)
        if i % 8 == 7:
            block = pl.ds(2 * (i - 7), 16)
            pltpu.make_async_copy(ob.at[block], out_hbm.at[0, block], osem).start()
    pltpu.make_async_copy(ob, out_hbm.at[0], osem).wait()


def decode(pos, lengths, x, w_in, b_in, b_mid, ss, ds, sd, w_mid):
    smem = pl.BlockSpec(memory_space=pltpu.SMEM)
    vmem = pl.BlockSpec(memory_space=pltpu.VMEM)
    hbm = pl.BlockSpec(memory_space=pl.ANY)
    return pl.pallas_call(
        main_body,
        in_specs=[smem, smem, vmem, vmem, vmem, vmem, vmem, vmem, hbm, hbm],
        out_specs=hbm,
        out_shape=jax.ShapeDtypeStruct((1, 2 * HT, 2 * WT, CH), BF),
        scratch_shapes=[
            pltpu.VMEM((3, HT * 8, 128), F32),
            pltpu.VMEM((5 * STRIP, HT + 16, 128), F32),
            pltpu.VMEM((9, 128, CH), BF),
            pltpu.VMEM((KIN, SW * CH), BF),
            pltpu.VMEM((9, TOP + MROW, 128), F32),
            pltpu.VMEM((MROW, KMID), BF),
            pltpu.VMEM((MROW, KMID), BF),
            pltpu.VMEM((MROW, KMID), BF),
            pltpu.VMEM((MROW, KMID), BF),
            pltpu.VMEM((KMID, 2 * CH), BF),
            pltpu.VMEM((4, KMID, CH), BF),
            pltpu.VMEM((3, HT * PITCH, 128), F32),
            pltpu.VMEM((6, HT * PITCH, 128), F32),
            pltpu.VMEM((6, MROW, 128), F32),
            pltpu.VMEM((12, MROW, 128), F32),
            pltpu.VMEM((3, 4, 2, 2 * WT, 128), F32),
            pltpu.VMEM((2 * HT, 2 * WT, CH), BF),
            pltpu.SemaphoreType.DMA((13,)),
            pltpu.SemaphoreType.DMA,
        ],
        compiler_params=pltpu.CompilerParams(vmem_limit_bytes=VMEM_LIMIT),
        name="decode",
    )(pos, lengths, x, w_in, b_in, b_mid, ss, ds, sd, w_mid)


def on_device(latents, lengths, w_in, b_in, w_mid, b_mid):
    groups = lax.axis_size("req")
    before = lax.ppermute(latents, "req", [(i, i + 1) for i in range(groups - 1)])
    x = lax.all_to_all(patch(before, slots(latents)), "tm", split_axis=0, concat_axis=0, tiled=True)
    w_mid = pltpu.with_memory_space_constraint(w_mid, pltpu.HBM)
    ss, ds, sd = prep(w_mid)
    sd = pltpu.with_memory_space_constraint(sd, pltpu.HBM)
    pos = lax.axis_index(("req", "tm")).astype(jnp.int32).reshape(1)
    return decode(pos, lengths, x, w_in.reshape(KIN, CH), b_in, b_mid, ss, ds, sd, w_mid)


def solution(mesh):
    in_specs = (P("req", "tm"), P(), P(), P(), P(), P())
    out_specs = P(("req", "tm"), None, None, None)
    return jax.shard_map(
        on_device, mesh=mesh, in_specs=in_specs, out_specs=out_specs, check_vma=False
    )
```

```python
import jax
import jax.numpy as jnp
from jax import lax
from jax.experimental import pallas as pl
from jax.experimental.pallas import tpu as pltpu
from jax.sharding import PartitionSpec as P

C = 16
HT = 32
WT = 24
CH = 384
BF = jnp.bfloat16
F32 = jnp.float32
KIN = 27 * C
KMID = 3 * CH
STRIP = 4
SW = WT // STRIP
VMEM_LIMIT = 44 * 2**20
PITCH = WT + 1
TOP = 32
HALF = HT // 2
FULL = HALF * PITCH
MORE = 432


def prep_body(w_hbm, ss_ref, sd_ref, by_col_hbm, mixed_hbm, w, by_col, mixed, isem, osem):
    rows = 128
    parts = [(t, slice(r, r + rows)) for t in range(3) for r in range(0, CH, rows)]
    reads, writes = [], []
    for n, (t, r) in enumerate(parts):
        cp = pltpu.make_async_copy(w_hbm.at[t, :, :, r], w.at[t, :, :, r], isem.at[n])
        cp.start()
        reads.append(cp)
    for n, (t, r) in enumerate(parts):
        reads[n].wait()
        out = slice(n * rows, (n + 1) * rows)
        row = [[w[t, p, q, r].astype(F32) for q in range(3)] for p in range(3)]
        cols = [[x[0] + x[1] + x[2] for x in row], [x[0] for x in row], [x[2] for x in row]]
        for k, (x, y, z) in enumerate(cols):
            upper, lower = x + y, y + z
            whole = (upper + z).astype(BF)
            if k == 0:
                ss_ref[out] = whole
                by_col[0, out, 0:CH] = x.astype(BF)
                by_col[0, out, CH : 2 * CH] = upper.astype(BF)
                by_col[1, out, 0:CH] = lower.astype(BF)
                by_col[1, out, CH : 2 * CH] = z.astype(BF)
            else:
                sd_ref[out, (k - 1) * CH : k * CH] = whole
                mixed[k - 1, out] = upper.astype(BF)
                mixed[k + 1, out] = lower.astype(BF)
        for k, (src, dst) in enumerate(((by_col, by_col_hbm), (mixed, mixed_hbm))):
            cp = pltpu.make_async_copy(src.at[:, out], dst.at[:, out], osem.at[k, n])
            cp.start()
            writes.append(cp)
    for cp in writes:
        cp.wait()


def prep(w_mid):
    vmem = pl.BlockSpec(memory_space=pltpu.VMEM)
    hbm = pl.BlockSpec(memory_space=pl.ANY)
    return pl.pallas_call(
        prep_body,
        in_specs=[hbm],
        out_specs=[vmem, vmem, hbm, hbm],
        out_shape=[
            jax.ShapeDtypeStruct((KMID, CH), BF),
            jax.ShapeDtypeStruct((KMID, 2 * CH), BF),
            pltpu.HBM((2, KMID, 2 * CH), BF),
            pltpu.HBM((4, KMID, CH), BF),
        ],
        scratch_shapes=[
            pltpu.VMEM((3, 3, 3, CH, CH), BF),
            pltpu.VMEM((2, KMID, 2 * CH), BF),
            pltpu.VMEM((4, KMID, CH), BF),
            pltpu.SemaphoreType.DMA((9,)),
            pltpu.SemaphoreType.DMA((2, 9)),
        ],
        compiler_params=pltpu.CompilerParams(vmem_limit_bytes=24 * 2**20),
        name="prep",
    )(w_mid)


def slots_body(own_ref, o_ref, rows, out):
    for c in range(3):
        lanes = slice(c * 128, (c + 1) * 128)
        rows[c, 0:8, :] = jnp.zeros((8, 128), F32)
        rows[c, 8 : 8 + HT, :] = own_ref[:, lanes].astype(F32)
        for k in range(8):
            piece = rows[c, 4 + k : 4 + k + HT, :] if k < 5 else jnp.zeros((HT, 128), F32)
            out[c, pl.ds(k, HT, stride=8), :] = piece
        o_ref[:, :, lanes] = out[c].reshape(HT, 8, 128).astype(BF)


def slots(own):
    return pl.pallas_call(
        slots_body,
        out_shape=jax.ShapeDtypeStruct((HT, 8, CH), BF),
        scratch_shapes=[pltpu.VMEM((3, HT + 8, 128), F32), pltpu.VMEM((3, HT * 8, 128), F32)],
        compiler_params=pltpu.CompilerParams(vmem_limit_bytes=8 * 2**20),
        name="slots",
    )(own)


def patch_body(before_ref, s_ref, o_ref):
    o_ref[4:HT] = s_ref[4:HT]
    tail = before_ref[...].astype(F32)[HT - 8 : HT]
    for d in range(4):
        here = s_ref[d].astype(F32)
        o_ref[d] = jnp.concatenate([tail[4 + d : 8], here[4 - d : 8]], axis=0).astype(BF)


def patch(before, own_slots):
    return pl.pallas_call(
        patch_body,
        out_shape=jax.ShapeDtypeStruct((HT, 8, CH), BF),
        compiler_params=pltpu.CompilerParams(vmem_limit_bytes=8 * 2**20),
        name="patch",
    )(before, own_slots)


def main_body(
    pos_ref, len_ref, x_ref, win_ref, bin_ref, bmid_ref, w_ss, w_sd, by_col_hbm, mixed_hbm,
    w_hbm, out_hbm, xf, xp, zt, at, even, odd, ls, lsd, lm, lmd, lp, lpd, w_by_col, w_m, w_p,
    r_ss, r_sd, r_ms, r_md, r_ps, r_pd, st, ob, wsem, osem,
):
    copy = pltpu.make_async_copy
    by_col = [copy(by_col_hbm.at[k], w_by_col.at[k], wsem.at[k]) for k in range(2)]
    both = []
    for k, (w, p) in enumerate(((w_m, 0), (w_p, 2))):
        for q in range(2):
            both.append(copy(mixed_hbm.at[2 * k + q], w.at[2 - p + q], wsem.at[2 + 2 * k + q]))
            for t in range(3):
                part = pl.ds(t * CH, CH)
                both.append(
                    copy(w_hbm.at[t, p, 2 * q], w.at[p + q, part], wsem.at[6 + 6 * k + 3 * q + t])
                )
    for cp in by_col:
        cp.start()

    first = pos_ref[0] - 4
    rid = [jnp.int32(0)] * 5
    end = jnp.int32(0)
    for r in range(8):
        end = end + len_ref[r]
        rid = [rid[k] + (first + k >= end).astype(jnp.int32) for k in range(5)]
    ok = lambda k, g: ((first + k >= 0) & (rid[k] == rid[g])).astype(F32)
    m_in = [[ok(g + t, g + 2) if t < 2 else None for t in range(3)] for g in range(3)]
    m_mid = [ok(2, 4), ok(3, 4), None]
    bias = lambda ref, c: ref[pl.ds(c * 128, 128)].reshape(1, 128)
    times = lambda v, m: v if m is None else v * m

    for c in range(3):
        xf[c] = x_ref[:, :, c * 128 : (c + 1) * 128].reshape(HT * 8, 128).astype(F32)
    for f in range(5):
        x = [0.5 * xf[c, pl.ds(f, HT, stride=8), :] for c in range(3)]
        x = jnp.concatenate([jnp.zeros((HT, C), F32)] + x + [jnp.zeros((HT, 128 - C), F32)], axis=1)
        for s in range(STRIP):
            k = f * STRIP + s
            xp[k, 0:8, :] = jnp.zeros((8, 128), F32)
            xp[k, 8 : 8 + HT, :] = x[:, s * SW * C : s * SW * C + 128]
            xp[k, 8 + HT : 16 + HT, :] = jnp.zeros((8, 128), F32)

    for t in range(3):
        for p in range(3):
            for b in range(3):
                block = []
                for k in range(4 * b, 4 * b + 4):
                    s, g = k // 3, k % 3
                    for first_row in (7 + p, 8 + p):
                        x = xp[(g + t) * STRIP + s, pl.ds(first_row, HALF, stride=2), :]
                        block.append(times(x, m_in[g][t]).astype(BF))
                z = jnp.concatenate(block, axis=0)
                zt[3 * t + p, :, b * 128 : (b + 1) * 128] = z.T

    for tp in range(9):
        for j in range(SW):
            at[tp * 48 : (tp + 1) * 48, j * CH : (j + 1) * CH] = zt[tp, 16 * j : 16 * j + 48, :]

    for k in range(9):
        for ref in (even, odd):
            ref[k, 0:TOP, :] = jnp.zeros((TOP, 128), F32)
            ref[k, pl.ds(TOP + WT, HALF, stride=PITCH), :] = jnp.zeros((HALF, 128), F32)
            ref[k, TOP + FULL : TOP + MORE, :] = jnp.zeros((MORE - FULL, 128), F32)

    for cp in both:
        cp.start()
    for n in range(SW // 2):
        a = at[:, n * 2 * CH : (n + 1) * 2 * CH]
        v = lax.dot_general(a, win_ref[...], (((0,), (0,)), ((), ())), preferred_element_type=F32)
        for k in range(2 * STRIP * 3):
            s, g, j = k // 3 % STRIP, k % 3, n * 2 + k // (3 * STRIP)
            for c in range(3):
                u = v[k * HT : (k + 1) * HT, c * 128 : (c + 1) * 128]
                u = u + 0.5 * bias(bin_ref, c)
                u = times(u * (1.0 + jnp.tanh(u)), m_mid[g]).astype(BF).astype(F32)
                to = pl.ds(TOP + s * SW + j, HALF, stride=PITCH)
                even[3 * g + c, to, :] = u[0:HALF]
                odd[3 * g + c, to, :] = u[HALF:HT]

    for cp in by_col:
        cp.wait()

    def build(plain, diff, value, rows, step):
        for k in range(9):
            lanes = slice(k * 128, (k + 1) * 128)
            for lo in range(0, rows, step):
                to = slice(lo, lo + step)
                here = value(k, lo, step)
                plain[to, lanes] = here.astype(BF)
                diff[to, lanes] = (here - value(k, lo - 1, step)).astype(BF)

    on_even = lambda k, lo, n: even[k, TOP + lo : TOP + lo + n, :]
    below = lambda k, lo, n: odd[k, TOP + lo : TOP + lo + n, :]
    def mm(out, first_chunk, lhs, w):
        v = jnp.dot(lhs[...], w, preferred_element_type=F32)
        for k in range(v.shape[1] // 128):
            part = v[:, k * 128 : (k + 1) * 128]
            out[first_chunk + k] = part + bias(bmid_ref, k) if out is r_ss else part

    build(ls, lsd, on_even, FULL, 80)
    mm(r_ss, 0, ls, w_ss[...])
    mm(r_sd, 0, lsd, w_sd[...])
    build(lm, lmd, lambda k, lo, n: below(k, lo - PITCH, n) - on_even(k, lo, n), MORE, 144)
    mm(r_ms, 0, lm, w_by_col[0])
    build(lp, lpd, lambda k, lo, n: below(k, lo, n) - on_even(k, lo, n), FULL, 80)
    mm(r_ps, 0, lp, w_by_col[1])
    for cp in both:
        cp.wait()

    def emit(m, c):
        at_row = lambda ref, k, off: ref[k, m * PITCH + off : m * PITCH + off + WT, :]
        slot = m % 4

        def columns(plain, diff, k):
            x = at_row(plain, 3 * k + c, 0)
            return x - at_row(diff, 4 * c + 2 * k, 0), x + at_row(diff, 4 * c + 2 * k + 1, 1)

        if m < HALF:
            x = at_row(r_ss, c, 0)
            base = x - at_row(r_sd, c, 0), x + at_row(r_sd, 3 + c, 1)
        else:
            base = bias(bmid_ref, c), bias(bmid_ref, c)
        rows = {4 * m - 1: (r_ms, r_md, 1), 4 * m: (r_ms, r_md, 0)}
        rows.update({4 * m + 1: (r_ps, r_pd, 1), 4 * m + 2: (r_ps, r_pd, 0)})
        for n, (u, (plain, diff, k)) in enumerate(rows.items()):
            if 0 <= u < 2 * HT and (m < HALF or n == 0):
                y = columns(plain, diff, k)
                for b in range(2):
                    st[c, slot, n, pl.ds(b, WT, stride=2), :] = base[b] + y[b]
                ob[u, :, c * 128 : (c + 1) * 128] = st[c, slot, n].astype(BF)

    def diff_part(c):
        for out, lhs, w in ((r_md, lmd, w_m), (r_pd, lpd, w_p)):
            weights = [w[k, :, c * 128 : (c + 1) * 128] for k in range(4)]
            mm(out, 4 * c, lhs, jnp.concatenate(weights, axis=1))

    def out_part(c):
        for m in range(HALF + 1):
            emit(m, c)
            if c == 2 and m % 4 == 0 and m > 0:
                block = pl.ds(4 * m - 16, 16)
                pltpu.make_async_copy(ob.at[block], out_hbm.at[0, block], osem).start()

    diff_part(0)
    diff_part(1)
    out_part(0)
    diff_part(2)
    out_part(1)
    out_part(2)
    pltpu.make_async_copy(ob, out_hbm.at[0], osem).wait()


def decode(pos, lengths, x, w_in, b_in, b_mid, ss, sd, by_col, mixed, w_mid):
    smem = pl.BlockSpec(memory_space=pltpu.SMEM)
    vmem = pl.BlockSpec(memory_space=pltpu.VMEM)
    hbm = pl.BlockSpec(memory_space=pl.ANY)
    return pl.pallas_call(
        main_body,
        in_specs=[smem, smem, vmem, vmem, vmem, vmem, vmem, vmem, hbm, hbm, hbm],
        out_specs=hbm,
        out_shape=jax.ShapeDtypeStruct((1, 2 * HT, 2 * WT, CH), BF),
        scratch_shapes=[
            pltpu.VMEM((3, HT * 8, 128), F32),
            pltpu.VMEM((5 * STRIP, HT + 16, 128), F32),
            pltpu.VMEM((9, 128, CH), BF),
            pltpu.VMEM((KIN, SW * CH), BF),
            pltpu.VMEM((9, TOP + MORE, 128), F32),
            pltpu.VMEM((9, TOP + MORE, 128), F32),
            pltpu.VMEM((FULL, KMID), BF),
            pltpu.VMEM((FULL, KMID), BF),
            pltpu.VMEM((MORE, KMID), BF),
            pltpu.VMEM((MORE, KMID), BF),
            pltpu.VMEM((FULL, KMID), BF),
            pltpu.VMEM((FULL, KMID), BF),
            pltpu.VMEM((2, KMID, 2 * CH), BF),
            pltpu.VMEM((4, KMID, CH), BF),
            pltpu.VMEM((4, KMID, CH), BF),
            pltpu.VMEM((3, FULL, 128), F32),
            pltpu.VMEM((6, FULL, 128), F32),
            pltpu.VMEM((6, MORE, 128), F32),
            pltpu.VMEM((12, MORE, 128), F32),
            pltpu.VMEM((6, FULL, 128), F32),
            pltpu.VMEM((12, FULL, 128), F32),
            pltpu.VMEM((3, 4, 4, 2 * WT, 128), F32),
            pltpu.VMEM((2 * HT, 2 * WT, CH), BF),
            pltpu.SemaphoreType.DMA((18,)),
            pltpu.SemaphoreType.DMA,
        ],
        compiler_params=pltpu.CompilerParams(vmem_limit_bytes=VMEM_LIMIT),
        name="decode",
    )(pos, lengths, x, w_in, b_in, b_mid, ss, sd, by_col, mixed, w_mid)


def on_device(latents, lengths, w_in, b_in, w_mid, b_mid):
    groups = lax.axis_size("req")
    before = lax.ppermute(latents, "req", [(i, i + 1) for i in range(groups - 1)])
    x = lax.all_to_all(patch(before, slots(latents)), "tm", split_axis=0, concat_axis=0, tiled=True)
    w_mid = pltpu.with_memory_space_constraint(w_mid, pltpu.HBM)
    ss, sd, by_col, mixed = prep(w_mid)
    by_col = pltpu.with_memory_space_constraint(by_col, pltpu.HBM)
    mixed = pltpu.with_memory_space_constraint(mixed, pltpu.HBM)
    pos = lax.axis_index(("req", "tm")).astype(jnp.int32).reshape(1)
    return decode(pos, lengths, x, w_in.reshape(KIN, CH), b_in, b_mid, ss, sd, by_col, mixed, w_mid)


def solution(mesh):
    in_specs = (P("req", "tm"), P(), P(), P(), P(), P())
    out_specs = P(("req", "tm"), None, None, None)
    return jax.shard_map(
        on_device, mesh=mesh, in_specs=in_specs, out_specs=out_specs, check_vma=False
    )
```

```python
import jax
import jax.numpy as jnp
from jax import lax
from jax.experimental import pallas as pl
from jax.experimental.pallas import tpu as pltpu
from jax.sharding import PartitionSpec as P

C = 16
HT = 32
WT = 24
CH = 384
BF = jnp.bfloat16
F32 = jnp.float32
KIN = 27 * C
KMID = 3 * CH
WINDOWS = 14
KPAIR = 640
GROUP = 3
VMEM_LIMIT = 44 * 2**20
PITCH = WT + 1
TOP = 32
HALF = HT // 2
FULL = HALF * PITCH
MORE = 432


def prep_body(w_hbm, ss_ref, sd_ref, by_col_hbm, mixed_hbm, w, by_col, mixed, isem, osem):
    rows = 128
    parts = [(t, slice(r, r + rows)) for t in range(3) for r in range(0, CH, rows)]
    reads, writes = [], []
    for n, (t, r) in enumerate(parts):
        cp = pltpu.make_async_copy(w_hbm.at[t, :, :, r], w.at[t, :, :, r], isem.at[n])
        cp.start()
        reads.append(cp)
    for n, (t, r) in enumerate(parts):
        reads[n].wait()
        out = slice(n * rows, (n + 1) * rows)
        row = [[w[t, p, q, r].astype(F32) for q in range(3)] for p in range(3)]
        cols = [[x[0] + x[1] + x[2] for x in row], [x[0] for x in row], [x[2] for x in row]]
        for k, (x, y, z) in enumerate(cols):
            upper, lower = x + y, y + z
            whole = (upper + z).astype(BF)
            if k == 0:
                ss_ref[out] = whole
                by_col[0, out, 0:CH] = x.astype(BF)
                by_col[0, out, CH : 2 * CH] = upper.astype(BF)
                by_col[1, out, 0:CH] = lower.astype(BF)
                by_col[1, out, CH : 2 * CH] = z.astype(BF)
            else:
                sd_ref[out, (k - 1) * CH : k * CH] = whole
                mixed[k - 1, out] = upper.astype(BF)
                mixed[k + 1, out] = lower.astype(BF)
        for k, (src, dst) in enumerate(((by_col, by_col_hbm), (mixed, mixed_hbm))):
            cp = pltpu.make_async_copy(src.at[:, out], dst.at[:, out], osem.at[k, n])
            cp.start()
            writes.append(cp)
    for cp in writes:
        cp.wait()


def prep(w_mid):
    vmem = pl.BlockSpec(memory_space=pltpu.VMEM)
    hbm = pl.BlockSpec(memory_space=pl.ANY)
    return pl.pallas_call(
        prep_body,
        in_specs=[hbm],
        out_specs=[vmem, vmem, hbm, hbm],
        out_shape=[
            jax.ShapeDtypeStruct((KMID, CH), BF),
            jax.ShapeDtypeStruct((KMID, 2 * CH), BF),
            pltpu.HBM((2, KMID, 2 * CH), BF),
            pltpu.HBM((4, KMID, CH), BF),
        ],
        scratch_shapes=[
            pltpu.VMEM((3, 3, 3, CH, CH), BF),
            pltpu.VMEM((2, KMID, 2 * CH), BF),
            pltpu.VMEM((4, KMID, CH), BF),
            pltpu.SemaphoreType.DMA((9,)),
            pltpu.SemaphoreType.DMA((2, 9)),
        ],
        compiler_params=pltpu.CompilerParams(vmem_limit_bytes=24 * 2**20),
        name="prep",
    )(w_mid)


def slots_body(own_ref, o_ref, rows, out):
    for c in range(3):
        lanes = slice(c * 128, (c + 1) * 128)
        rows[c, 0:8, :] = jnp.zeros((8, 128), F32)
        rows[c, 8 : 8 + HT, :] = own_ref[:, lanes].astype(F32)
        for k in range(8):
            piece = rows[c, 4 + k : 4 + k + HT, :] if k < 5 else jnp.zeros((HT, 128), F32)
            out[c, pl.ds(k, HT, stride=8), :] = piece
        o_ref[:, :, lanes] = out[c].reshape(HT, 8, 128).astype(BF)


def slots(own):
    return pl.pallas_call(
        slots_body,
        out_shape=jax.ShapeDtypeStruct((HT, 8, CH), BF),
        scratch_shapes=[pltpu.VMEM((3, HT + 8, 128), F32), pltpu.VMEM((3, HT * 8, 128), F32)],
        compiler_params=pltpu.CompilerParams(vmem_limit_bytes=8 * 2**20),
        name="slots",
    )(own)


def patch_body(before_ref, s_ref, o_ref):
    o_ref[4:HT] = s_ref[4:HT]
    tail = before_ref[...].astype(F32)[HT - 8 : HT]
    for d in range(4):
        here = s_ref[d].astype(F32)
        o_ref[d] = jnp.concatenate([tail[4 + d : 8], here[4 - d : 8]], axis=0).astype(BF)


def patch(before, own_slots):
    return pl.pallas_call(
        patch_body,
        out_shape=jax.ShapeDtypeStruct((HT, 8, CH), BF),
        compiler_params=pltpu.CompilerParams(vmem_limit_bytes=8 * 2**20),
        name="patch",
    )(before, own_slots)


def main_body(
    pos_ref, len_ref, x_ref, win_ref, bin_ref, bmid_ref, w_ss, w_sd, by_col_hbm, mixed_hbm,
    w_hbm, out_hbm, xf, xp, wb, at, even, odd, ls, lsd, lm, lmd, lp, lpd, w_by_col, w_m, w_p,
    r_ss, r_sd, r_ms, r_md, r_ps, r_pd, st, ob, wsem, osem,
):
    copy = pltpu.make_async_copy
    by_col = [copy(by_col_hbm.at[k], w_by_col.at[k], wsem.at[k]) for k in range(2)]
    both = []
    for k, (w, p) in enumerate(((w_m, 0), (w_p, 2))):
        for q in range(2):
            both.append(copy(mixed_hbm.at[2 * k + q], w.at[2 - p + q], wsem.at[2 + 2 * k + q]))
            for t in range(3):
                part = pl.ds(t * CH, CH)
                both.append(
                    copy(w_hbm.at[t, p, 2 * q], w.at[p + q, part], wsem.at[6 + 6 * k + 3 * q + t])
                )
    for cp in by_col:
        cp.start()

    first = pos_ref[0] - 4
    rid = [jnp.int32(0)] * 5
    end = jnp.int32(0)
    for r in range(8):
        end = end + len_ref[r]
        rid = [rid[k] + (first + k >= end).astype(jnp.int32) for k in range(5)]
    ok = lambda k, g: ((first + k >= 0) & (rid[k] == rid[g])).astype(F32)
    m_in = [[ok(g + t, g + 2) if t < 2 else None for t in range(3)] for g in range(3)]
    m_mid = [ok(2, 4), ok(3, 4), None]
    bias = lambda ref, c: ref[pl.ds(c * 128, 128)].reshape(1, 128)
    times = lambda v, m: v if m is None else v * m

    for c in range(3):
        xf[c] = x_ref[:, :, c * 128 : (c + 1) * 128].reshape(HT * 8, 128).astype(F32)
    for f in range(5):
        x = [0.5 * xf[c, pl.ds(f, HT, stride=8), :] for c in range(3)]
        left, right = jnp.zeros((HT, 64 + C), F32), jnp.zeros((HT, 160 + C), F32)
        x = jnp.concatenate([left] + x + [right], axis=1)
        for n in range(WINDOWS):
            k = f * WINDOWS + n
            xp[k, 0:8, :] = jnp.zeros((8, 128), F32)
            xp[k, 8 : 8 + HT, :] = x[:, 32 * n : 32 * n + 128]
            xp[k, 8 + HT : 16 + HT, :] = jnp.zeros((8, 128), F32)

    wb[...] = jnp.zeros((KPAIR, 2 * CH), BF)
    for tp in range(9):
        taps = win_ref[tp * 48 : (tp + 1) * 48, :]
        wb[tp * 64 : tp * 64 + 48, 0:CH] = taps
        wb[tp * 64 + 16 : tp * 64 + 64, CH : 2 * CH] = taps

    for cp in both:
        cp.start()

    for k in range(9):
        for ref in (even, odd):
            ref[k, 0:TOP, :] = jnp.zeros((TOP, 128), F32)
            ref[k, pl.ds(TOP + WT, HALF, stride=PITCH), :] = jnp.zeros((HALF, 128), F32)
            ref[k, TOP + FULL : TOP + MORE, :] = jnp.zeros((MORE - FULL, 128), F32)

    low = lax.broadcasted_iota(jnp.int32, (1, 128), 1) < 64
    scale = lambda m: jnp.float32(1) if m is None else m
    mask = [
        [
            jnp.where(low, scale(m_in[g][2 * n // 3]), scale(m_in[g][(2 * n + 1) // 3]) if n < 4 else 0.0)
            for n in range(5)
        ]
        for g in range(3)
    ]

    def window(tp, g, s, par, n):
        t, p = tp // 3, tp % 3
        return xp[(g + t) * WINDOWS + s + n, pl.ds(7 + p + par, HALF, stride=2), :]

    per = 3 * HT
    for s in range(WT // 2):
        for g in range(3):
            for par in range(2):
                row = s * per + g * HT + par * HALF
                for n in range(5):
                    y = window(2 * n, g, s, par, 2)
                    if n < 4:
                        y = jnp.where(low, y, window(2 * n + 1, g, s, par, 0))
                    at[row : row + HALF, n * 128 : (n + 1) * 128] = (y * mask[g][n]).astype(BF)
        if s % GROUP == GROUP - 1:
            rows = slice((s + 1 - GROUP) * per, (s + 1) * per)
            v = jnp.dot(at[rows, :], wb[...], preferred_element_type=F32)
            for k in range(GROUP * 6):
                s2, g, par = s + 1 - GROUP + k // 6, k // 2 % 3, k % 2
                ref = (even, odd)[par]
                for q in range(6):
                    j, c = q // 3, q % 3
                    u = v[k * HALF : (k + 1) * HALF, q * 128 : (q + 1) * 128]
                    u = u + 0.5 * bias(bin_ref, c)
                    u = times(u * (1.0 + jnp.tanh(u)), m_mid[g]).astype(BF).astype(F32)
                    ref[3 * g + c, pl.ds(TOP + 2 * s2 + j, HALF, stride=PITCH), :] = u

    for cp in by_col:
        cp.wait()

    def build(plain, diff, value, rows, step):
        for k in range(9):
            lanes = slice(k * 128, (k + 1) * 128)
            for lo in range(0, rows, step):
                to = slice(lo, lo + step)
                here = value(k, lo, step)
                plain[to, lanes] = here.astype(BF)
                diff[to, lanes] = (here - value(k, lo - 1, step)).astype(BF)

    on_even = lambda k, lo, n: even[k, TOP + lo : TOP + lo + n, :]
    below = lambda k, lo, n: odd[k, TOP + lo : TOP + lo + n, :]
    def mm(out, first_chunk, lhs, w):
        v = jnp.dot(lhs[...], w, preferred_element_type=F32)
        for k in range(v.shape[1] // 128):
            part = v[:, k * 128 : (k + 1) * 128]
            out[first_chunk + k] = part + bias(bmid_ref, k) if out is r_ss else part

    build(ls, lsd, on_even, FULL, 80)
    mm(r_ss, 0, ls, w_ss[...])
    mm(r_sd, 0, lsd, w_sd[...])
    build(lm, lmd, lambda k, lo, n: below(k, lo - PITCH, n) - on_even(k, lo, n), MORE, 144)
    mm(r_ms, 0, lm, w_by_col[0])
    build(lp, lpd, lambda k, lo, n: below(k, lo, n) - on_even(k, lo, n), FULL, 80)
    mm(r_ps, 0, lp, w_by_col[1])
    for cp in both:
        cp.wait()

    def emit(m, c, plain, diff):
        at_row = lambda ref, k, off: ref[k, m * PITCH + off : m * PITCH + off + WT, :]

        def columns(k):
            x = at_row(plain, 3 * k + c, 0)
            return x - at_row(diff, 4 * c + 2 * k, 0), x + at_row(diff, 4 * c + 2 * k + 1, 1)

        if m < HALF:
            x = at_row(r_ss, c, 0)
            base = x - at_row(r_sd, c, 0), x + at_row(r_sd, 3 + c, 1)
        else:
            base = bias(bmid_ref, c), bias(bmid_ref, c)
        pair = ((4 * m - 1, 1), (4 * m, 0)) if plain is r_ms else ((4 * m + 1, 1), (4 * m + 2, 0))
        for u, k in pair:
            if 0 <= u < 2 * HT:
                y = columns(k)
                n = u % 16
                for b in range(2):
                    st[c, n, pl.ds(b, WT, stride=2), :] = base[b] + y[b]
                ob[u, :, c * 128 : (c + 1) * 128] = st[c, n].astype(BF)

    def diff_part(c, out, lhs, w):
        weights = [w[k, :, c * 128 : (c + 1) * 128] for k in range(4)]
        mm(out, 4 * c, lhs, jnp.concatenate(weights, axis=1))

    m_part = lambda c: diff_part(c, r_md, lmd, w_m)
    p_part = lambda c: diff_part(c, r_pd, lpd, w_p)

    def m_out(c):
        for m in range(HALF + 1):
            emit(m, c, r_ms, r_md)

    def p_out(c):
        for m in range(HALF):
            emit(m, c, r_ps, r_pd)
            if c == 2 and m % 2 == 1:
                block = pl.ds(4 * m - 4, 8)
                pltpu.make_async_copy(ob.at[block], out_hbm.at[0, block], osem).start()

    m_part(0)
    p_part(0)
    m_part(1)
    m_out(0)
    p_part(1)
    p_out(0)
    m_part(2)
    m_out(1)
    p_part(2)
    p_out(1)
    m_out(2)
    p_out(2)
    pltpu.make_async_copy(ob, out_hbm.at[0], osem).wait()


def decode(pos, lengths, x, w_in, b_in, b_mid, ss, sd, by_col, mixed, w_mid):
    smem = pl.BlockSpec(memory_space=pltpu.SMEM)
    vmem = pl.BlockSpec(memory_space=pltpu.VMEM)
    hbm = pl.BlockSpec(memory_space=pl.ANY)
    return pl.pallas_call(
        main_body,
        in_specs=[smem, smem, vmem, vmem, vmem, vmem, vmem, vmem, hbm, hbm, hbm],
        out_specs=hbm,
        out_shape=jax.ShapeDtypeStruct((1, 2 * HT, 2 * WT, CH), BF),
        scratch_shapes=[
            pltpu.VMEM((3, HT * 8, 128), F32),
            pltpu.VMEM((5 * WINDOWS, HT + 16, 128), F32),
            pltpu.VMEM((KPAIR, 2 * CH), BF),
            pltpu.VMEM((3 * HT * WT // 2, KPAIR), BF),
            pltpu.VMEM((9, TOP + MORE, 128), F32),
            pltpu.VMEM((9, TOP + MORE, 128), F32),
            pltpu.VMEM((FULL, KMID), BF),
            pltpu.VMEM((FULL, KMID), BF),
            pltpu.VMEM((MORE, KMID), BF),
            pltpu.VMEM((MORE, KMID), BF),
            pltpu.VMEM((FULL, KMID), BF),
            pltpu.VMEM((FULL, KMID), BF),
            pltpu.VMEM((2, KMID, 2 * CH), BF),
            pltpu.VMEM((4, KMID, CH), BF),
            pltpu.VMEM((4, KMID, CH), BF),
            pltpu.VMEM((3, FULL, 128), F32),
            pltpu.VMEM((6, FULL, 128), F32),
            pltpu.VMEM((6, MORE, 128), F32),
            pltpu.VMEM((12, MORE, 128), F32),
            pltpu.VMEM((6, FULL, 128), F32),
            pltpu.VMEM((12, FULL, 128), F32),
            pltpu.VMEM((3, 16, 2 * WT, 128), F32),
            pltpu.VMEM((2 * HT, 2 * WT, CH), BF),
            pltpu.SemaphoreType.DMA((18,)),
            pltpu.SemaphoreType.DMA,
        ],
        compiler_params=pltpu.CompilerParams(vmem_limit_bytes=VMEM_LIMIT),
        name="decode",
    )(pos, lengths, x, w_in, b_in, b_mid, ss, sd, by_col, mixed, w_mid)


def on_device(latents, lengths, w_in, b_in, w_mid, b_mid):
    groups = lax.axis_size("req")
    before = lax.ppermute(latents, "req", [(i, i + 1) for i in range(groups - 1)])
    x = lax.all_to_all(patch(before, slots(latents)), "tm", split_axis=0, concat_axis=0, tiled=True)
    w_mid = pltpu.with_memory_space_constraint(w_mid, pltpu.HBM)
    ss, sd, by_col, mixed = prep(w_mid)
    by_col = pltpu.with_memory_space_constraint(by_col, pltpu.HBM)
    mixed = pltpu.with_memory_space_constraint(mixed, pltpu.HBM)
    pos = lax.axis_index(("req", "tm")).astype(jnp.int32).reshape(1)
    return decode(pos, lengths, x, w_in.reshape(KIN, CH), b_in, b_mid, ss, sd, by_col, mixed, w_mid)


def solution(mesh):
    in_specs = (P("req", "tm"), P(), P(), P(), P(), P())
    out_specs = P(("req", "tm"), None, None, None)
    return jax.shard_map(
        on_device, mesh=mesh, in_specs=in_specs, out_specs=out_specs, check_vma=False
    )
```

```python
import jax
import jax.numpy as jnp
from jax import lax
from jax.experimental import pallas as pl
from jax.experimental.pallas import tpu as pltpu
from jax.sharding import PartitionSpec as P

C = 16
HT = 32
WT = 24
CH = 384
BF = jnp.bfloat16
F32 = jnp.float32
KIN = 27 * C
KMID = 3 * CH
WINDOWS = 14
KPAIR = 640
ENDS = (3, 6, 9, 11)
VMEM_LIMIT = 44 * 2**20
PITCH = WT + 1
TOP = 32
HALF = HT // 2
FULL = HALF * PITCH
MORE = 432


def prep_body(w_hbm, ss_ref, sd_ref, by_col_hbm, mixed_hbm, w, by_col, mixed, isem, osem):
    rows = 128
    parts = [(t, slice(r, r + rows)) for t in range(3) for r in range(0, CH, rows)]
    reads, writes = [], []
    for n, (t, r) in enumerate(parts):
        cp = pltpu.make_async_copy(w_hbm.at[t, :, :, r], w.at[t, :, :, r], isem.at[n])
        cp.start()
        reads.append(cp)
    for n, (t, r) in enumerate(parts):
        reads[n].wait()
        out = slice(n * rows, (n + 1) * rows)
        row = [[w[t, p, q, r].astype(F32) for q in range(3)] for p in range(3)]
        cols = [[x[0] + x[1] + x[2] for x in row], [x[0] for x in row], [x[2] for x in row]]
        for k, (x, y, z) in enumerate(cols):
            upper, lower = x + y, y + z
            whole = (upper + z).astype(BF)
            if k == 0:
                ss_ref[out] = whole
                by_col[0, out, 0:CH] = x.astype(BF)
                by_col[0, out, CH : 2 * CH] = upper.astype(BF)
                by_col[1, out, 0:CH] = lower.astype(BF)
                by_col[1, out, CH : 2 * CH] = z.astype(BF)
            else:
                sd_ref[out, (k - 1) * CH : k * CH] = whole
                mixed[k - 1, out] = upper.astype(BF)
                mixed[k + 1, out] = lower.astype(BF)
        for k, (src, dst) in enumerate(((by_col, by_col_hbm), (mixed, mixed_hbm))):
            cp = pltpu.make_async_copy(src.at[:, out], dst.at[:, out], osem.at[k, n])
            cp.start()
            writes.append(cp)
    for cp in writes:
        cp.wait()


def prep(w_mid):
    vmem = pl.BlockSpec(memory_space=pltpu.VMEM)
    hbm = pl.BlockSpec(memory_space=pl.ANY)
    return pl.pallas_call(
        prep_body,
        in_specs=[hbm],
        out_specs=[vmem, vmem, hbm, hbm],
        out_shape=[
            jax.ShapeDtypeStruct((KMID, CH), BF),
            jax.ShapeDtypeStruct((KMID, 2 * CH), BF),
            pltpu.HBM((2, KMID, 2 * CH), BF),
            pltpu.HBM((4, KMID, CH), BF),
        ],
        scratch_shapes=[
            pltpu.VMEM((3, 3, 3, CH, CH), BF),
            pltpu.VMEM((2, KMID, 2 * CH), BF),
            pltpu.VMEM((4, KMID, CH), BF),
            pltpu.SemaphoreType.DMA((9,)),
            pltpu.SemaphoreType.DMA((2, 9)),
        ],
        compiler_params=pltpu.CompilerParams(vmem_limit_bytes=24 * 2**20),
        name="prep",
    )(w_mid)


def slots_body(own_ref, o_ref, rows, out):
    for c in range(3):
        lanes = slice(c * 128, (c + 1) * 128)
        rows[c, 0:8, :] = jnp.zeros((8, 128), F32)
        rows[c, 8 : 8 + HT, :] = own_ref[:, lanes].astype(F32)
        for k in range(8):
            piece = rows[c, 4 + k : 4 + k + HT, :] if k < 5 else jnp.zeros((HT, 128), F32)
            out[c, pl.ds(k, HT, stride=8), :] = piece
        o_ref[:, :, lanes] = out[c].reshape(HT, 8, 128).astype(BF)


def slots(own):
    return pl.pallas_call(
        slots_body,
        out_shape=jax.ShapeDtypeStruct((HT, 8, CH), BF),
        scratch_shapes=[pltpu.VMEM((3, HT + 8, 128), F32), pltpu.VMEM((3, HT * 8, 128), F32)],
        compiler_params=pltpu.CompilerParams(vmem_limit_bytes=8 * 2**20),
        name="slots",
    )(own)


def patch_body(before_ref, s_ref, o_ref):
    o_ref[4:HT] = s_ref[4:HT]
    tail = before_ref[...].astype(F32)[HT - 8 : HT]
    for d in range(4):
        here = s_ref[d].astype(F32)
        o_ref[d] = jnp.concatenate([tail[4 + d : 8], here[4 - d : 8]], axis=0).astype(BF)


def patch(before, own_slots):
    return pl.pallas_call(
        patch_body,
        out_shape=jax.ShapeDtypeStruct((HT, 8, CH), BF),
        compiler_params=pltpu.CompilerParams(vmem_limit_bytes=8 * 2**20),
        name="patch",
    )(before, own_slots)


def main_body(
    pos_ref, len_ref, x_ref, win_ref, bin_ref, bmid_ref, w_ss, w_sd, by_col_hbm, mixed_hbm,
    w_hbm, out_hbm, xf, xp, wb, at, even, odd, ls, lsd, lm, lmd, lp, lpd, w_by_col, w_m, w_p,
    r_ss, r_sd, r_ms, r_md, r_ps, r_pd, st, ob, wsem, osem,
):
    copy = pltpu.make_async_copy
    by_col = [copy(by_col_hbm.at[k], w_by_col.at[k], wsem.at[k]) for k in range(2)]
    both = []
    for k, (w, p) in enumerate(((w_m, 0), (w_p, 2))):
        for q in range(2):
            both.append(copy(mixed_hbm.at[2 * k + q], w.at[2 - p + q], wsem.at[2 + 2 * k + q]))
            for t in range(3):
                part = pl.ds(t * CH, CH)
                both.append(
                    copy(w_hbm.at[t, p, 2 * q], w.at[p + q, part], wsem.at[6 + 6 * k + 3 * q + t])
                )
    for cp in by_col:
        cp.start()

    first = pos_ref[0] - 4
    rid = [jnp.int32(0)] * 5
    end = jnp.int32(0)
    for r in range(8):
        end = end + len_ref[r]
        rid = [rid[k] + (first + k >= end).astype(jnp.int32) for k in range(5)]
    ok = lambda k, g: ((first + k >= 0) & (rid[k] == rid[g])).astype(F32)
    m_in = [[ok(g + t, g + 2) if t < 2 else None for t in range(3)] for g in range(3)]
    m_mid = [ok(2, 4), ok(3, 4), None]
    bias = lambda ref, c: ref[pl.ds(c * 128, 128)].reshape(1, 128)
    times = lambda v, m: v if m is None else v * m

    for c in range(3):
        xf[c] = x_ref[:, :, c * 128 : (c + 1) * 128].reshape(HT * 8, 128).astype(F32)
    for f in range(5):
        x = [0.5 * xf[c, pl.ds(f, HT, stride=8), :] for c in range(3)]
        left, right = jnp.zeros((HT, 64 + C), F32), jnp.zeros((HT, 160 + C), F32)
        x = jnp.concatenate([left] + x + [right], axis=1)
        for n in range(WINDOWS):
            k = f * WINDOWS + n
            xp[k, 0:8, :] = jnp.zeros((8, 128), F32)
            xp[k, 8 : 8 + HT, :] = x[:, 32 * n : 32 * n + 128]
            xp[k, 8 + HT : 16 + HT, :] = jnp.zeros((8, 128), F32)

    wb[...] = jnp.zeros((KPAIR, 2 * CH), BF)
    for tp in range(9):
        taps = win_ref[tp * 48 : (tp + 1) * 48, :]
        wb[tp * 64 : tp * 64 + 48, 0:CH] = taps
        wb[tp * 64 + 16 : tp * 64 + 64, CH : 2 * CH] = taps

    for cp in both:
        cp.start()

    for k in range(9):
        for ref in (even, odd):
            ref[k, 0:TOP, :] = jnp.zeros((TOP, 128), F32)
            ref[k, pl.ds(TOP + WT, HALF, stride=PITCH), :] = jnp.zeros((HALF, 128), F32)
            ref[k, TOP + FULL : TOP + MORE, :] = jnp.zeros((MORE - FULL, 128), F32)

    low = lax.broadcasted_iota(jnp.int32, (1, 128), 1) < 64
    scale = lambda m: jnp.float32(1) if m is None else m
    mask = [
        [
            jnp.where(low, scale(m_in[g][2 * n // 3]), scale(m_in[g][(2 * n + 1) // 3]) if n < 4 else 0.0)
            for n in range(5)
        ]
        for g in range(3)
    ]

    def window(tp, g, s, par, n):
        t, p = tp // 3, tp % 3
        return xp[(g + t) * WINDOWS + s + n, pl.ds(7 + p + par, HALF, stride=2), :]

    per = 3 * HT
    for s in range(WT // 2):
        for g in range(3):
            for par in range(2):
                row = s * per + g * HT + par * HALF
                for n in range(5):
                    y = window(2 * n, g, s, par, 2)
                    if n < 4:
                        y = jnp.where(low, y, window(2 * n + 1, g, s, par, 0))
                    at[row : row + HALF, n * 128 : (n + 1) * 128] = (y * mask[g][n]).astype(BF)
        if s in ENDS:
            group = s - max([e for e in ENDS if e < s], default=-1)
            rows = slice((s + 1 - group) * per, (s + 1) * per)
            v = jnp.dot(at[rows, :], wb[...], preferred_element_type=F32)
            for k in range(group * 6):
                s2, g, par = s + 1 - group + k // 6, k // 2 % 3, k % 2
                ref = (even, odd)[par]
                for q in range(6):
                    j, c = q // 3, q % 3
                    u = v[k * HALF : (k + 1) * HALF, q * 128 : (q + 1) * 128]
                    u = u + 0.5 * bias(bin_ref, c)
                    u = times(u * (1.0 + jnp.tanh(u)), m_mid[g]).astype(BF).astype(F32)
                    ref[3 * g + c, pl.ds(TOP + 2 * s2 + j, HALF, stride=PITCH), :] = u

    for cp in by_col:
        cp.wait()

    def build(plain, diff, value, rows, step):
        for k in range(9):
            lanes = slice(k * 128, (k + 1) * 128)
            for lo in range(0, rows, step):
                to = slice(lo, lo + step)
                here = value(k, lo, step)
                plain[to, lanes] = here.astype(BF)
                diff[to, lanes] = (here - value(k, lo - 1, step)).astype(BF)

    on_even = lambda k, lo, n: even[k, TOP + lo : TOP + lo + n, :]
    below = lambda k, lo, n: odd[k, TOP + lo : TOP + lo + n, :]
    def mm(out, first_chunk, lhs, w):
        v = jnp.dot(lhs[...], w, preferred_element_type=F32)
        for k in range(v.shape[1] // 128):
            part = v[:, k * 128 : (k + 1) * 128]
            out[first_chunk + k] = part + bias(bmid_ref, k) if out is r_ss else part

    build(ls, lsd, on_even, FULL, 80)
    mm(r_ss, 0, ls, w_ss[...])
    mm(r_sd, 0, lsd, w_sd[...])
    build(lm, lmd, lambda k, lo, n: below(k, lo - PITCH, n) - on_even(k, lo, n), MORE, 144)
    mm(r_ms, 0, lm, w_by_col[0])
    build(lp, lpd, lambda k, lo, n: below(k, lo, n) - on_even(k, lo, n), FULL, 80)
    mm(r_ps, 0, lp, w_by_col[1])
    for cp in both:
        cp.wait()

    def emit(m, c, plain, diff):
        at_row = lambda ref, k, off: ref[k, m * PITCH + off : m * PITCH + off + WT, :]

        def columns(k):
            x = at_row(plain, 3 * k + c, 0)
            return x - at_row(diff, 4 * c + 2 * k, 0), x + at_row(diff, 4 * c + 2 * k + 1, 1)

        if m < HALF:
            x = at_row(r_ss, c, 0)
            base = x - at_row(r_sd, c, 0), x + at_row(r_sd, 3 + c, 1)
        else:
            base = bias(bmid_ref, c), bias(bmid_ref, c)
        pair = ((4 * m - 1, 1), (4 * m, 0)) if plain is r_ms else ((4 * m + 1, 1), (4 * m + 2, 0))
        for u, k in pair:
            if 0 <= u < 2 * HT:
                y = columns(k)
                n = u % 16
                for b in range(2):
                    st[c, n, pl.ds(b, WT, stride=2), :] = base[b] + y[b]
                ob[u, :, c * 128 : (c + 1) * 128] = st[c, n].astype(BF)

    def diff_part(c, out, lhs, w):
        weights = [w[k, :, c * 128 : (c + 1) * 128] for k in range(4)]
        mm(out, 4 * c, lhs, jnp.concatenate(weights, axis=1))

    m_part = lambda c: diff_part(c, r_md, lmd, w_m)
    p_part = lambda c: diff_part(c, r_pd, lpd, w_p)

    def m_out(c):
        for m in range(HALF + 1):
            emit(m, c, r_ms, r_md)

    def p_out(c):
        for m in range(HALF):
            emit(m, c, r_ps, r_pd)
            if c == 2:
                block = pl.ds(4 * m, 4)
                pltpu.make_async_copy(ob.at[block], out_hbm.at[0, block], osem).start()

    m_part(0)
    p_part(0)
    m_part(1)
    m_out(0)
    p_part(1)
    p_out(0)
    m_part(2)
    m_out(1)
    p_part(2)
    p_out(1)
    m_out(2)
    p_out(2)
    pltpu.make_async_copy(ob, out_hbm.at[0], osem).wait()


def decode(pos, lengths, x, w_in, b_in, b_mid, ss, sd, by_col, mixed, w_mid):
    smem = pl.BlockSpec(memory_space=pltpu.SMEM)
    vmem = pl.BlockSpec(memory_space=pltpu.VMEM)
    hbm = pl.BlockSpec(memory_space=pl.ANY)
    return pl.pallas_call(
        main_body,
        in_specs=[smem, smem, vmem, vmem, vmem, vmem, vmem, vmem, hbm, hbm, hbm],
        out_specs=hbm,
        out_shape=jax.ShapeDtypeStruct((1, 2 * HT, 2 * WT, CH), BF),
        scratch_shapes=[
            pltpu.VMEM((3, HT * 8, 128), F32),
            pltpu.VMEM((5 * WINDOWS, HT + 16, 128), F32),
            pltpu.VMEM((KPAIR, 2 * CH), BF),
            pltpu.VMEM((3 * HT * WT // 2, KPAIR), BF),
            pltpu.VMEM((9, TOP + MORE, 128), F32),
            pltpu.VMEM((9, TOP + MORE, 128), F32),
            pltpu.VMEM((FULL, KMID), BF),
            pltpu.VMEM((FULL, KMID), BF),
            pltpu.VMEM((MORE, KMID), BF),
            pltpu.VMEM((MORE, KMID), BF),
            pltpu.VMEM((FULL, KMID), BF),
            pltpu.VMEM((FULL, KMID), BF),
            pltpu.VMEM((2, KMID, 2 * CH), BF),
            pltpu.VMEM((4, KMID, CH), BF),
            pltpu.VMEM((4, KMID, CH), BF),
            pltpu.VMEM((3, FULL, 128), F32),
            pltpu.VMEM((6, FULL, 128), F32),
            pltpu.VMEM((6, MORE, 128), F32),
            pltpu.VMEM((12, MORE, 128), F32),
            pltpu.VMEM((6, FULL, 128), F32),
            pltpu.VMEM((12, FULL, 128), F32),
            pltpu.VMEM((3, 16, 2 * WT, 128), F32),
            pltpu.VMEM((2 * HT, 2 * WT, CH), BF),
            pltpu.SemaphoreType.DMA((18,)),
            pltpu.SemaphoreType.DMA,
        ],
        compiler_params=pltpu.CompilerParams(vmem_limit_bytes=VMEM_LIMIT),
        name="decode",
    )(pos, lengths, x, w_in, b_in, b_mid, ss, sd, by_col, mixed, w_mid)


def on_device(latents, lengths, w_in, b_in, w_mid, b_mid):
    groups = lax.axis_size("req")
    before = lax.ppermute(latents, "req", [(i, i + 1) for i in range(groups - 1)])
    x = lax.all_to_all(patch(before, slots(latents)), "tm", split_axis=0, concat_axis=0, tiled=True)
    w_mid = pltpu.with_memory_space_constraint(w_mid, pltpu.HBM)
    ss, sd, by_col, mixed = prep(w_mid)
    by_col = pltpu.with_memory_space_constraint(by_col, pltpu.HBM)
    mixed = pltpu.with_memory_space_constraint(mixed, pltpu.HBM)
    pos = lax.axis_index(("req", "tm")).astype(jnp.int32).reshape(1)
    return decode(pos, lengths, x, w_in.reshape(KIN, CH), b_in, b_mid, ss, sd, by_col, mixed, w_mid)


def solution(mesh):
    in_specs = (P("req", "tm"), P(), P(), P(), P(), P())
    out_specs = P(("req", "tm"), None, None, None)
    return jax.shard_map(
        on_device, mesh=mesh, in_specs=in_specs, out_specs=out_specs, check_vma=False
    )
```
